32 devices in a mesh: ctx: 8 (over y, x, core), kvh: 4 (over z).
Axes of the slice: x: 2, y: 2, z: 4, core: 2. Of those that a mesh axis runs over, the one named last changes fastest.
Arguments:
- queries: float32 [8, 256, 64, 128], P('ctx', None, 'kvh'), may hold values from -64 to 64
- cache_keys: float32 [8, 4096, 128], P('kvh', 'ctx'), may hold values from -16 to 16
- cache_values: float32 [8, 4096, 128], P('kvh', 'ctx'), may hold values from -6 to 6
- bounds: int32 [8, 3], replicated, may hold values from 0 to 2048, as said below
Outputs:
- attended: float32 [8, 256, 64, 128], P('ctx', None, 'kvh')
The draws below stay inside these ranges and needn't reach their ends.
Inputs may be any that keep to these rules, and one draw needn't show every extreme that they name: bounds[b] = (s, w, l) with 2 <= s <= 64, 0 <= w < 256, 1792 < l <= 2048; block 0 has s = 64, w = 0, l = 2048.
All inputs are finite; a program needn't handle non-finite values.
Results may differ from the reference program's by a relative error of at most 0.0003.
Values sent between devices are 32-bit elements; how exact they have to be, the bound alone decides.
No kernel may reach another device: no remote copies, remote signals or barrier semaphores. Data moves between devices by JAX's collectives and lax.ppermute only.
A program may use at most 64 MiB of HBM per device.

```python
import math
import jax
import jax.numpy as jnp
from jax import lax

HEADS = 64
KVH = 8
HD = 128
QB = 256
ROWS = 512
SINK = 64
BLOCKS = 8
TOTAL = 4096
N_CTX = 8


def shared_keys(key):
    keys = jax.random.normal(jax.random.fold_in(key, 7), (KVH, TOTAL, HD), jnp.float32)
    return jnp.clip(keys, -16.0, 16.0)


def draw_cache_keys(key, part):
    return shared_keys(key)


def draw_queries(key, part):
    values = 2.0 * jax.random.normal(jax.random.fold_in(key, 13), (BLOCKS, QB, HEADS, HD), jnp.float32)
    return jnp.clip(values, -64.0, 64.0)


def draw_bounds(key, part):
    sink_end = jax.random.randint(jax.random.fold_in(key, 21), (BLOCKS,), 2, SINK + 1)
    window_start = jax.random.randint(jax.random.fold_in(key, 22), (BLOCKS,), 0, ROWS // 2)
    valid_end = 4 * ROWS - jax.random.randint(jax.random.fold_in(key, 23), (BLOCKS,), 0, ROWS // 2)
    sink_end = sink_end.at[0].set(SINK)
    window_start = window_start.at[0].set(0)
    valid_end = valid_end.at[0].set(4 * ROWS)
    return jnp.stack([sink_end, window_start, valid_end], axis=1).astype(jnp.int32)


def levels(rng, shape, pieces, least, top_value):
    def one(position, blocks):
        draws = jax.random.uniform(jax.random.fold_in(jax.random.fold_in(rng, 6), position), (blocks,), jnp.float32, least / len(pieces), top_value / len(pieces))
        return jnp.repeat(jnp.exp(draws), shape[position] // blocks).reshape((-1,) + (1,) * (len(shape) - position - 1))

    factor_of = one(*pieces[0])
    for cut in pieces[1:]:
        factor_of = factor_of * one(*cut)
    return factor_of


def normal_values(key, shape, deviation, most, shards=(), held_as=jnp.bfloat16):
    drawn = deviation * jax.random.normal(key, shape, jnp.float32)
    if shards:
        drawn = drawn * levels(key, shape, shards, -0.22, 0.18)
    return jnp.clip(drawn, -most, most).astype(held_as)


def setup_inputs(seed: int = 0) -> dict:
    key_of = jax.random.split(jax.random.key(seed), 5)
    return {
        "queries": draw_queries(jax.random.fold_in(key_of[4], 71), 0),
        "cache_keys": draw_cache_keys(jax.random.fold_in(key_of[4], 71), 0),
        "cache_values": normal_values(key_of[2], (KVH, TOTAL, HD), 1.0, 6.0, ((0, 4), (1, 8)), jnp.float32),
        "bounds": draw_bounds(jax.random.fold_in(key_of[4], 71), 0),
    }


NEG = -1e+30

def reference(queries, cache_keys, cache_values, bounds):
    total = ROWS * N_CTX
    group = HEADS // KVH
    scale = 1.0 / math.sqrt(HD)
    ext_keys = jnp.concatenate([cache_keys, cache_keys[:, :4 * ROWS]], axis=1)
    ext_values = jnp.concatenate([cache_values, cache_values[:, :4 * ROWS]], axis=1)

    def one(block):
        query = lax.dynamic_index_in_dim(queries, block, 0, keepdims=False).reshape(QB, KVH, group, HD)
        limits = lax.dynamic_index_in_dim(bounds, block, 0, keepdims=False)
        start = (block * ROWS).astype(jnp.int32)
        span_keys = lax.dynamic_slice_in_dim(ext_keys, start, 4 * ROWS, 1)
        span_values = lax.dynamic_slice_in_dim(ext_values, start, 4 * ROWS, 1)
        keys = jnp.concatenate([cache_keys[:, :SINK], span_keys], axis=1)
        values = jnp.concatenate([cache_values[:, :SINK], span_values], axis=1)
        offsets = jnp.arange(4 * ROWS, dtype=jnp.int32)
        span_mask = (offsets >= limits[1]) & (offsets < limits[2])
        slots = jnp.arange(SINK, dtype=jnp.int32)
        rel = (slots - start) % total
        sink_mask = (slots < limits[0]) & jnp.logical_not((rel >= limits[1]) & (rel < limits[2]))
        mask = jnp.concatenate([sink_mask, span_mask])
        scores = jnp.einsum('qkgd,ksd->kgqs', query, keys, precision=lax.Precision.HIGHEST) * scale
        masked = jnp.where(mask, scores, NEG)
        top = lax.optimization_barrier(jnp.max(masked, axis=-1, keepdims=True))
        weights = jnp.where(mask, jnp.exp(masked - top), 0.0)
        totals = lax.optimization_barrier(jnp.sum(weights, axis=-1))
        mixed = jnp.einsum('kgqs,ksd->kgqd', weights, values, precision=lax.Precision.HIGHEST)
        mixed = mixed / totals[..., None]
        return jnp.transpose(mixed, (2, 0, 1, 3)).reshape(QB, HEADS, HD)
    return lax.map(one, jnp.arange(BLOCKS, dtype=jnp.int32))
```

```python
import functools
import math

import jax
import jax.numpy as jnp
from jax import lax
from jax.experimental import pallas as pl
from jax.experimental.pallas import tpu as pltpu
from jax.sharding import PartitionSpec as P

SINK = 64
SPAN = 4
LANES = 128
BLOCK_ROWS = 1024
VMEM_LIMIT = 20 << 20
PACK_LIMIT = 58 << 20
NEG = -1e30


BF16 = jnp.bfloat16
F32 = jnp.float32
VMEM = pl.BlockSpec(memory_space=pltpu.VMEM)
SMEM = pl.BlockSpec(memory_space=pltpu.SMEM)
HBM = pl.BlockSpec(memory_space=pltpu.HBM)
ANY = pl.BlockSpec(memory_space=pl.ANY)


def split(x):
    high = x.astype(BF16)
    return high, (x - high.astype(F32)).astype(BF16)


def exchange(x, source, count):
    return lax.ppermute(x, "ctx", [(source(i) % count, i) for i in range(count)])


def first_source(i):
    return i + (4, 2, -1, 3)[i % 4]


def second_source(i):
    return i + (3, 4, 4, -3)[i % 4]


def pair_source(i):
    return i ^ 1


PIECES = (
    (("own_pair", 1), ("first", 2), ("own_pair", 1), ("first", 3)),
    (("first_pair", 3), ("first_pair", 3), ("second", 3), ("second", 1)),
    (("second", 2), ("second_pair", 1), ("second_pair", 2), ("second_pair", 2)),
)


def pick(role, values):
    result = values[0]
    for r in range(1, len(values)):
        result = jnp.where(role == r, values[r], result)
    return result


def make_step(*, jobs, pieces, sink, fresh, final, rows_t, group, head_size, slots, total):
    names = list(dict.fromkeys(n for piece in pieces for n, _ in piece))
    rows = rows_t * group
    block = min(BLOCK_ROWS, rows)
    block_t = block // group
    chunks = rows // block
    width = slots * len(pieces)
    scale = math.log2(math.e) / math.sqrt(head_size)
    count = len(jobs)

    def kernel(*refs):
        refs = list(refs)

        def take(n):
            front, refs[:] = refs[:n], refs[n:]
            return front

        place_ref, bounds_ref, q_ref = take(3)
        sources = {n: take(2 if fresh else count) for n in names}

        def source(job, name, j):
            return sources[name][job][j]

        sink_refs = [take(count) for _ in range(sink)]
        states_in = [take(2) for _ in jobs] if not fresh else None
        if final == 2:
            take(1)
        if final:
            (out_ref,) = take(1)
        else:
            states_out = [take(2) for _ in jobs]
        (sink_out,) = take(1) if fresh else (None,)
        k_cat, v_cat = take(2)
        ks_cat, vs_cat = take(2) if sink else (None, None)
        o_buf, o_sem = take(2) if final else (None, None)
        loads = {}
        if fresh:
            kv_buf, sems = take(2)
            for job, head in enumerate(jobs):
                loads[job] = [
                    pltpu.make_async_copy(ref.at[head], kv_buf.at[job, j], sems.at[job, j])
                    for j, ref in enumerate(sources["self"])
                ]
                for copy in loads[job]:
                    copy.start()
            sources = {"self": [kv_buf.at[job] for job in range(count)]}

        place = place_ref[0]
        role = lax.rem(place, 4)
        first, lower, upper = (bounds_ref[j, place] for j in range(3))
        lanes_half = lax.broadcasted_iota(jnp.int32, (1, LANES), 1) < SINK

        def load(job, piece, j):
            own_names = list(dict.fromkeys(n for n, _ in piece))
            value = source(job, own_names[0], j)
            for name in own_names[1:]:
                chosen = functools.reduce(jnp.logical_or, [role == r for r in range(4) if piece[r][0] == name])
                value = jnp.where(chosen, source(job, name, j), value)
            return value

        def prepare(job):
            for number, piece in enumerate(pieces):
                part = slice(number * slots, (number + 1) * slots)
                distance = pick(role, [d for _, d in piece])
                offset = distance * slots + lax.broadcasted_iota(jnp.int32, (slots, LANES), 0)
                lane = lax.broadcasted_iota(jnp.int32, (slots, LANES), 1)
                hidden = (lane == 0) & ((offset < lower) | (offset >= upper))
                high, low = split(load(job, piece, 0))
                mask = jnp.where(hidden, NEG, 0.0).astype(BF16)
                for j, value in enumerate((high, high, low, mask)):
                    k_cat[job, part, j * LANES : (j + 1) * LANES] = value
                for j, value in enumerate(split(load(job, piece, 1))):
                    v_cat[job, part, j * LANES : (j + 1) * LANES] = value
            if sink:

                def load_sink(j):
                    value = sink_refs[0][job][j, :SINK]
                    for r in range(1, sink):
                        value = jnp.where(place == r + 1, sink_refs[r][job][j, :SINK], value)
                    return value

                slot = lax.rem(lax.broadcasted_iota(jnp.int32, (2 * SINK, LANES), 0), SINK)
                lane = lax.broadcasted_iota(jnp.int32, (2 * SINK, LANES), 1)
                behind = slot - place * slots
                behind = jnp.where(behind < 0, behind + total, behind)
                seen = (slot < first) & ((behind < lower) | (behind >= upper))
                mask = jnp.where((lane == 0) & jnp.logical_not(seen), NEG, 0.0).astype(BF16)
                high, low = (jnp.concatenate([x, x]) for x in split(load_sink(0)))
                for j, value in enumerate((high, high, low, mask)):
                    ks_cat[job, :, j * LANES : (j + 1) * LANES] = value
                zero = jnp.zeros((SINK, LANES), BF16)
                high, low = split(load_sink(1))
                for j, value in enumerate(((high, high), (low, zero))):
                    vs_cat[job, :, j * LANES : (j + 1) * LANES] = jnp.concatenate(value)

        def scores_of(query, keys):
            return lax.dot_general(query, keys, (((1,), (1,)), ((), ())), preferred_element_type=F32)

        def mix(weights, values):
            return lax.dot_general(weights, values, (((1,), (0,)), ((), ())), preferred_element_type=F32)

        def by_halves(product, left, right):
            half = left.shape[0] // 2
            return jnp.concatenate([product(left[:half], right), product(left[half:], right)])

        def groups(x):
            return [x[:, j * LANES : (j + 1) * LANES] for j in range(width // LANES)]

        copies = []
        for job, head in enumerate(jobs):
            for copy in loads.get(job, ()):
                copy.wait()
            if fresh:
                for j in range(2):
                    sink_out[job, j] = source(job, "self", j)[:SINK]
            prepare(job)
            for chunk in range(chunks):
                here = pl.ds(chunk * block, block)
                query = q_ref[pl.ds(chunk * block_t, block_t), head * group : (head + 1) * group]
                high, low = split(query.reshape(block, head_size) * scale)
                ones = jnp.ones((block, LANES), BF16)
                query = jnp.concatenate([high, low, high, ones], axis=1)
                scores = scores_of(query, k_cat[job])
                top = functools.reduce(jnp.maximum, groups(scores))
                if sink:
                    sink_scores = by_halves(scores_of, query, ks_cat[job])
                    top = jnp.maximum(top, sink_scores)
                top = jnp.max(top, axis=1, keepdims=True)
                if fresh:
                    top = jnp.broadcast_to(top, (block, LANES))
                else:
                    old_top = states_in[job][1][here, :LANES]
                    top = jnp.maximum(top, old_top)
                    shrink = jnp.exp2(old_top - top)
                weights = jnp.exp2(scores - jnp.tile(top, (1, width // LANES)))
                sums = functools.reduce(jnp.add, groups(weights))
                high, low = split(weights)
                mixed = mix(high, v_cat[job])
                if sink:
                    weights = jnp.exp2(sink_scores - top)
                    sums = sums + jnp.where(lanes_half, weights, 0.0)
                    rest = weights - weights.astype(BF16).astype(F32)
                    mixed = mixed + by_halves(mix, jnp.where(lanes_half, weights, rest).astype(BF16), vs_cat[job])
                mixed = mixed[:, :LANES] + mixed[:, LANES:] + mix(low, v_cat[job, :, :LANES])
                if not fresh:
                    sums = sums + states_in[job][1][here, LANES:] * shrink
                    mixed = mixed + states_in[job][0][here] * shrink
                if final:
                    sums = jnp.sum(sums, axis=1, keepdims=True)
                    o_buf[chunk] = (mixed / sums).reshape(block_t, group, head_size)
                    copy = pltpu.make_async_copy(
                        o_buf.at[chunk],
                        out_ref.at[pl.ds(chunk * block_t, block_t), pl.ds(head * group, group)],
                        o_sem.at[chunk],
                    )
                    copy.start()
                    copies.append(copy)
                else:
                    acc_out, stat_out = states_out[job]
                    acc_out[here] = mixed
                    stat_out[here, :LANES] = top
                    stat_out[here, LANES:] = sums
        for copy in copies:
            copy.wait()

    taken = 2 if fresh else len(names) * count + count * sink + 2 * count
    in_specs = [SMEM, SMEM, VMEM] + [ANY if fresh else VMEM] * taken
    in_specs += [ANY] * (final == 2)
    scratch = [pltpu.VMEM((count, width, 4 * LANES), BF16), pltpu.VMEM((count, width, 2 * LANES), BF16)]
    if sink:
        scratch += [pltpu.VMEM((count, 2 * SINK, n * LANES), BF16) for n in (4, 2)]
    if final:
        scratch += [pltpu.VMEM((chunks, block_t, group, head_size), F32), pltpu.SemaphoreType.DMA((chunks,))]

    if fresh:
        scratch += [pltpu.VMEM((count, 2, slots, head_size), F32), pltpu.SemaphoreType.DMA((count, 2))]

    def call(queries, *args):
        if final:
            out_shape, out_specs = jax.ShapeDtypeStruct(queries.shape, F32), ANY
        else:
            out_shape = [
                jax.ShapeDtypeStruct((rows, head_size), F32),
                jax.ShapeDtypeStruct((rows, 2 * LANES), F32),
            ] * count
            out_specs = [VMEM, VMEM] * count
            if fresh:
                out_shape.append(jax.ShapeDtypeStruct((count, 2, SINK, head_size), F32))
                out_specs.append(VMEM)
        return pl.pallas_call(
            kernel,
            out_shape=out_shape,
            in_specs=in_specs,
            out_specs=out_specs,
            scratch_shapes=scratch,
            input_output_aliases={len(in_specs) - 1: 0} if final == 2 else {},
            compiler_params=pltpu.CompilerParams(vmem_limit_bytes=VMEM_LIMIT),
            cost_estimate=pl.CostEstimate(
                flops=count * rows * width * 2048, bytes_accessed=4 << 20, transcendentals=count * rows * width
            ),
        )(*args[:2], queries, *args[2:])

    return names, call


def pass_on(place, pair, came):
    def kernel(place_ref, pair_ref, came_ref, out_ref):
        out_ref[...] = jnp.where(lax.rem(place_ref[0], 4) == 3, pair_ref[...], came_ref[...])

    return pl.pallas_call(
        kernel,
        out_shape=jax.ShapeDtypeStruct(came.shape, F32),
        in_specs=[SMEM, VMEM, VMEM],
        out_specs=VMEM,
        compiler_params=pltpu.CompilerParams(vmem_limit_bytes=4 << 20),
        cost_estimate=pl.CostEstimate(flops=0, bytes_accessed=2 << 20, transcendentals=0),
    )(place, pair, came)


def pack(keys, values):
    heads, slots, head_size = keys.shape

    def kernel(k_ref, v_ref, *refs):
        outs, (buf, sems) = refs[:heads], refs[heads:]
        parts = [(h, j, ref) for h in range(heads) for j, ref in enumerate((k_ref, v_ref))]
        loads = [pltpu.make_async_copy(ref.at[h], buf.at[h, j], sems.at[h, j, 0]) for h, j, ref in parts]
        stores = [pltpu.make_async_copy(buf.at[h, j], outs[h].at[j], sems.at[h, j, 1]) for h, j, _ in parts]
        for load in loads:
            load.start()
        for load, store in zip(loads, stores):
            load.wait()
            store.start()
        for store in stores:
            store.wait()

    return pl.pallas_call(
        kernel,
        out_shape=[jax.ShapeDtypeStruct((2, slots, head_size), F32)] * heads,
        in_specs=[ANY, ANY],
        out_specs=[ANY] * heads,
        scratch_shapes=[pltpu.VMEM((heads, 2, slots, head_size), F32), pltpu.SemaphoreType.DMA((heads, 2, 2))],
        compiler_params=pltpu.CompilerParams(vmem_limit_bytes=PACK_LIMIT),
        cost_estimate=pl.CostEstimate(flops=8 << 30, bytes_accessed=8, transcendentals=0),
    )(keys, values)


def body(queries, cache_keys, cache_values, bounds):
    count = lax.axis_size("ctx")
    if count % 4:
        raise ValueError("ctx % 4")
    local_heads, slots, head_size = cache_keys.shape
    rows_t, query_heads = queries.shape[1:3]
    place = lax.axis_index("ctx").astype(jnp.int32)
    sizes = dict(
        rows_t=rows_t,
        group=query_heads // local_heads,
        head_size=head_size,
        slots=slots,
        total=slots * count,
    )
    heads = range(local_heads)
    heads = tuple(range(local_heads))
    scalars = (place.reshape(1), bounds.T)

    def step(jobs, pieces, sinks, fresh, final, *rest):
        names, call = make_step(jobs=jobs, pieces=pieces, sink=len(sinks), fresh=fresh, final=final, **sizes)
        taken = [got[n][h] for n in names for h in jobs] + [choice[h] for choice in sinks for h in jobs]
        if fresh:
            taken = [cache_keys, cache_values]
        return call(queries[0], *scalars, *taken, *rest)

    def send(arrays, source):
        moved = []
        for x in arrays:
            moved.append(exchange(x, source, count))
        return moved

    own = pack(cache_keys, cache_values)
    got = {"self": own}
    got["first"] = send(own, first_source)
    *flat, own_sinks = step(heads, ((("self", 0),) * 4,), (), True, 0)
    got["own_pair"] = send(own, pair_source)
    sinks = [own_sinks]
    if count == 8:
        far = send(sinks, lambda i: i ^ (4 if i % 2 else 2))
        near = send(far, pair_source)
        sink_args = (got["own_pair"], far[0], near[0], got["first"])
    else:
        have = 1
        while have <= count - SPAN:
            moved = send(sinks, lambda i, by=have: i - by)
            sinks = [jnp.where((place >= have) & (place < 2 * have), moved[0], sinks[0])]
            have *= 2
        sink_args = (sinks[0],)
    passed = []
    for h in heads:
        passed.append(pass_on(scalars[0], got["own_pair"][h], got["first"][h]))
    got["second"] = send(passed, second_source)
    got["first_pair"] = send(got["first"], pair_source)
    got["second_pair"] = send(got["second"], pair_source)
    for h in heads:
        here = slice(2 * h, 2 * h + 2)
        flat[here] = step((h,), PIECES[:1], (), False, 0, *flat[here])
    out = ()
    for h in heads:
        state, pieces = flat[2 * h : 2 * h + 2], PIECES[1:]
        if h < heads[-1]:
            state, pieces = step((h,), pieces[:1], (), False, 0, *state), pieces[1:]
        out = (step((h,), pieces, sink_args, False, 2 if h else 1, *state, *out),)
    return out[0][None]


def solution(mesh):
    placed = (P("ctx", None, "kvh", None), P("kvh", "ctx", None), P("kvh", "ctx", None), P())
    return jax.shard_map(body, mesh=mesh, in_specs=placed, out_specs=P("ctx", None, "kvh", None), check_vma=False)
```

```python
import functools
import math

import jax
import jax.numpy as jnp
from jax import lax
from jax.experimental import pallas as pl
from jax.experimental.pallas import tpu as pltpu
from jax.sharding import PartitionSpec as P

SINK = 64
SPAN = 4
LANES = 128
BLOCK_ROWS = 1024
OUT_PARTS = 8
VMEM_LIMIT = 20 << 20
PACK_LIMIT = 58 << 20
NEG = -1e30


BF16 = jnp.bfloat16
F32 = jnp.float32
VMEM = pl.BlockSpec(memory_space=pltpu.VMEM)
SMEM = pl.BlockSpec(memory_space=pltpu.SMEM)
HBM = pl.BlockSpec(memory_space=pltpu.HBM)
ANY = pl.BlockSpec(memory_space=pl.ANY)


def split(x):
    high = x.astype(BF16)
    return high, (x - high.astype(F32)).astype(BF16)


def exchange(x, source, count):
    return lax.ppermute(x, "ctx", [(source(i) % count, i) for i in range(count)])


def first_source(i):
    return i + (4, 2, -1, 3)[i % 4]


def second_source(i):
    return i + (3, 4, 4, -3)[i % 4]


def pair_source(i):
    return i ^ 1


PIECES = (
    (("own_pair", 1), ("first", 2), ("own_pair", 1), ("first", 3)),
    (("first_pair", 3), ("first_pair", 3), ("second", 3), ("second", 1)),
    (("second", 2), ("second_pair", 1), ("second_pair", 2), ("second_pair", 2)),
)


def pick(role, values):
    result = values[0]
    for r in range(1, len(values)):
        result = jnp.where(role == r, values[r], result)
    return result


def make_step(*, jobs, pieces, sink, fresh, final, rows_t, group, head_size, slots, total):
    names = list(dict.fromkeys(n for piece in pieces for n, _ in piece))
    rows = rows_t * group
    block = min(BLOCK_ROWS, rows)
    block_t = block // group
    chunks = rows // block
    width = slots * len(pieces)
    scale = math.log2(math.e) / math.sqrt(head_size)
    count = len(jobs)

    def kernel(*refs):
        refs = list(refs)

        def take(n):
            front, refs[:] = refs[:n], refs[n:]
            return front

        place_ref, bounds_ref, q_ref = take(3)
        sources = {n: take(count) for n in names}

        def source(job, name, j):
            return sources[name][job][j]

        sink_refs = [take(count) for _ in range(sink)]
        states_in = [take(2) for _ in jobs] if not fresh else None
        if final == 2:
            take(1)
        if final:
            (out_ref,) = take(1)
        else:
            states_out = [take(2) for _ in jobs]
        (sink_out,) = take(1) if fresh else (None,)
        k_cat, v_cat = take(2)
        ks_cat, vs_cat = take(2) if sink else (None, None)
        o_buf, o_sem = take(2) if final else (None, None)
        place = place_ref[0]
        role = lax.rem(place, 4)
        first, lower, upper = (bounds_ref[j, place] for j in range(3))
        lanes_half = lax.broadcasted_iota(jnp.int32, (1, LANES), 1) < SINK

        def load(job, piece, j):
            own_names = list(dict.fromkeys(n for n, _ in piece))
            value = source(job, own_names[0], j)
            for name in own_names[1:]:
                chosen = functools.reduce(jnp.logical_or, [role == r for r in range(4) if piece[r][0] == name])
                value = jnp.where(chosen, source(job, name, j), value)
            return value

        def prepare(job):
            for number, piece in enumerate(pieces):
                part = slice(number * slots, (number + 1) * slots)
                distance = pick(role, [d for _, d in piece])
                offset = distance * slots + lax.broadcasted_iota(jnp.int32, (slots, LANES), 0)
                lane = lax.broadcasted_iota(jnp.int32, (slots, LANES), 1)
                hidden = (lane == 0) & ((offset < lower) | (offset >= upper))
                high, low = split(load(job, piece, 0))
                mask = jnp.where(hidden, NEG, 0.0).astype(BF16)
                for j, value in enumerate((high, high, low, mask)):
                    k_cat[job, part, j * LANES : (j + 1) * LANES] = value
                for j, value in enumerate(split(load(job, piece, 1))):
                    v_cat[job, part, j * LANES : (j + 1) * LANES] = value
            if sink:

                def load_sink(j):
                    value = sink_refs[0][job][j, :SINK]
                    for r in range(1, sink):
                        value = jnp.where(place == r + 1, sink_refs[r][job][j, :SINK], value)
                    return value

                slot = lax.rem(lax.broadcasted_iota(jnp.int32, (2 * SINK, LANES), 0), SINK)
                lane = lax.broadcasted_iota(jnp.int32, (2 * SINK, LANES), 1)
                behind = slot - place * slots
                behind = jnp.where(behind < 0, behind + total, behind)
                seen = (slot < first) & ((behind < lower) | (behind >= upper))
                mask = jnp.where((lane == 0) & jnp.logical_not(seen), NEG, 0.0).astype(BF16)
                high, low = (jnp.concatenate([x, x]) for x in split(load_sink(0)))
                for j, value in enumerate((high, high, low, mask)):
                    ks_cat[job, :, j * LANES : (j + 1) * LANES] = value
                zero = jnp.zeros((SINK, LANES), BF16)
                high, low = split(load_sink(1))
                for j, value in enumerate(((high, high), (low, zero))):
                    vs_cat[job, :, j * LANES : (j + 1) * LANES] = jnp.concatenate(value)

        def scores_of(query, keys):
            return lax.dot_general(query, keys, (((1,), (1,)), ((), ())), preferred_element_type=F32)

        def mix(weights, values):
            return lax.dot_general(weights, values, (((1,), (0,)), ((), ())), preferred_element_type=F32)

        def by_halves(product, left, right):
            half = left.shape[0] // 2
            return jnp.concatenate([product(left[:half], right), product(left[half:], right)])

        def groups(x):
            return [x[:, j * LANES : (j + 1) * LANES] for j in range(width // LANES)]

        copies = []
        for job, head in enumerate(jobs):
            if fresh:
                for j in range(2):
                    sink_out[job, j] = source(job, "self", j)[:SINK]
            prepare(job)
            for chunk in range(chunks):
                here = pl.ds(chunk * block, block)
                query = q_ref[pl.ds(chunk * block_t, block_t), head * group : (head + 1) * group]
                high, low = split(query.reshape(block, head_size) * scale)
                ones = jnp.ones((block, LANES), BF16)
                query = jnp.concatenate([high, low, high, ones], axis=1)
                scores = scores_of(query, k_cat[job])
                top = functools.reduce(jnp.maximum, groups(scores))
                if sink:
                    sink_scores = by_halves(scores_of, query, ks_cat[job])
                    top = jnp.maximum(top, sink_scores)
                top = jnp.max(top, axis=1, keepdims=True)
                if fresh:
                    top = jnp.broadcast_to(top, (block, LANES))
                else:
                    old_top = states_in[job][1][here, :LANES]
                    top = jnp.maximum(top, old_top)
                    shrink = jnp.exp2(old_top - top)
                weights = jnp.exp2(scores - jnp.tile(top, (1, width // LANES)))
                sums = functools.reduce(jnp.add, groups(weights))
                high, low = split(weights)
                mixed = mix(high, v_cat[job])
                if sink:
                    weights = jnp.exp2(sink_scores - top)
                    sums = sums + jnp.where(lanes_half, weights, 0.0)
                    rest = weights - weights.astype(BF16).astype(F32)
                    mixed = mixed + by_halves(mix, jnp.where(lanes_half, weights, rest).astype(BF16), vs_cat[job])
                mixed = mixed[:, :LANES] + mixed[:, LANES:] + mix(low, v_cat[job, :, :LANES])
                if not fresh:
                    sums = sums + states_in[job][1][here, LANES:] * shrink
                    mixed = mixed + states_in[job][0][here] * shrink
                if final:
                    sums = jnp.sum(sums, axis=1, keepdims=True)
                    part_t = block_t // OUT_PARTS
                    for part in range(OUT_PARTS):
                        rows_of = slice(part * part_t * group, (part + 1) * part_t * group)
                        value = mixed[rows_of] / sums[rows_of]
                        o_buf[chunk, part] = value.reshape(part_t, group, head_size)
                        copy = pltpu.make_async_copy(
                            o_buf.at[chunk, part],
                            out_ref.at[pl.ds(chunk * block_t + part * part_t, part_t), pl.ds(head * group, group)],
                            o_sem.at[chunk, part],
                        )
                        copy.start()
                        copies.append(copy)
                else:
                    acc_out, stat_out = states_out[job]
                    acc_out[here] = mixed
                    stat_out[here, :LANES] = top
                    stat_out[here, LANES:] = sums
        for copy in copies:
            copy.wait()

    taken = len(names) * count + count * sink + 2 * count * (not fresh)
    in_specs = [SMEM, SMEM, VMEM] + [VMEM] * taken
    in_specs += [ANY] * (final == 2)
    scratch = [pltpu.VMEM((count, width, 4 * LANES), BF16), pltpu.VMEM((count, width, 2 * LANES), BF16)]
    if sink:
        scratch += [pltpu.VMEM((count, 2 * SINK, n * LANES), BF16) for n in (4, 2)]
    if final:
        shape = (chunks, OUT_PARTS, block_t // OUT_PARTS, group, head_size)
        scratch += [pltpu.VMEM(shape, F32), pltpu.SemaphoreType.DMA((chunks, OUT_PARTS))]

    def call(queries, *args):
        if final:
            out_shape, out_specs = jax.ShapeDtypeStruct(queries.shape, F32), ANY
        else:
            out_shape = [
                jax.ShapeDtypeStruct((rows, head_size), F32),
                jax.ShapeDtypeStruct((rows, 2 * LANES), F32),
            ] * count
            out_specs = [VMEM, VMEM] * count
            if fresh:
                out_shape.append(jax.ShapeDtypeStruct((count, 2, SINK, head_size), F32))
                out_specs.append(VMEM)
        return pl.pallas_call(
            kernel,
            out_shape=out_shape,
            in_specs=in_specs,
            out_specs=out_specs,
            scratch_shapes=scratch,
            input_output_aliases={len(in_specs) - 1: 0} if final == 2 else {},
            compiler_params=pltpu.CompilerParams(vmem_limit_bytes=VMEM_LIMIT),
            cost_estimate=pl.CostEstimate(
                flops=count * rows * width * 2048, bytes_accessed=4 << 20, transcendentals=count * rows * width
            ),
        )(*args[:2], queries, *args[2:])

    return names, call


def pass_on(place, pair, came):
    def kernel(place_ref, pair_ref, came_ref, out_ref):
        out_ref[...] = jnp.where(lax.rem(place_ref[0], 4) == 3, pair_ref[...], came_ref[...])

    return pl.pallas_call(
        kernel,
        out_shape=jax.ShapeDtypeStruct(came.shape, F32),
        in_specs=[SMEM, VMEM, VMEM],
        out_specs=VMEM,
        compiler_params=pltpu.CompilerParams(vmem_limit_bytes=4 << 20),
        cost_estimate=pl.CostEstimate(flops=0, bytes_accessed=2 << 20, transcendentals=0),
    )(place, pair, came)


def pack(keys, values):
    heads, slots, head_size = keys.shape

    def kernel(k_ref, v_ref, *refs):
        outs, (buf, sems) = refs[:heads], refs[heads:]
        parts = [(h, j, ref) for h in range(heads) for j, ref in enumerate((k_ref, v_ref))]
        loads = [pltpu.make_async_copy(ref.at[h], buf.at[h, j], sems.at[h, j, 0]) for h, j, ref in parts]
        stores = [pltpu.make_async_copy(buf.at[h, j], outs[h].at[j], sems.at[h, j, 1]) for h, j, _ in parts]
        for load in loads:
            load.start()
        for load, store in zip(loads, stores):
            load.wait()
            store.start()
        for store in stores:
            store.wait()

    return pl.pallas_call(
        kernel,
        out_shape=[jax.ShapeDtypeStruct((2, slots, head_size), F32)] * heads,
        in_specs=[ANY, ANY],
        out_specs=[ANY] * heads,
        scratch_shapes=[pltpu.VMEM((heads, 2, slots, head_size), F32), pltpu.SemaphoreType.DMA((heads, 2, 2))],
        compiler_params=pltpu.CompilerParams(vmem_limit_bytes=PACK_LIMIT),
        cost_estimate=pl.CostEstimate(flops=8 << 30, bytes_accessed=8, transcendentals=0),
    )(keys, values)


def body(queries, cache_keys, cache_values, bounds):
    count = lax.axis_size("ctx")
    if count % 4:
        raise ValueError("ctx % 4")
    local_heads, slots, head_size = cache_keys.shape
    rows_t, query_heads = queries.shape[1:3]
    place = lax.axis_index("ctx").astype(jnp.int32)
    sizes = dict(
        rows_t=rows_t,
        group=query_heads // local_heads,
        head_size=head_size,
        slots=slots,
        total=slots * count,
    )
    heads = range(local_heads)
    heads = tuple(range(local_heads))
    scalars = (place.reshape(1), bounds.T)

    def step(jobs, pieces, sinks, fresh, final, *rest):
        names, call = make_step(jobs=jobs, pieces=pieces, sink=len(sinks), fresh=fresh, final=final, **sizes)
        taken = [got[n][h] for n in names for h in jobs] + [choice[h] for choice in sinks for h in jobs]
        return call(queries[0], *scalars, *taken, *rest)

    def send(arrays, source):
        moved = []
        for x in arrays:
            moved.append(exchange(x, source, count))
        return moved

    own = pack(cache_keys, cache_values)
    got = {"self": own}
    got["first"] = send(own, first_source)
    *flat, own_sinks = step(heads, ((("self", 0),) * 4,), (), True, 0)
    got["own_pair"] = send(own, pair_source)
    sinks = [own_sinks]
    if count == 8:
        far = send(sinks, lambda i: i ^ (4 if i % 2 else 2))
        near = send(far, pair_source)
        sink_args = (got["own_pair"], far[0], near[0], got["first"])
    else:
        have = 1
        while have <= count - SPAN:
            moved = send(sinks, lambda i, by=have: i - by)
            sinks = [jnp.where((place >= have) & (place < 2 * have), moved[0], sinks[0])]
            have *= 2
        sink_args = (sinks[0],)
    passed = []
    for h in heads:
        passed.append(pass_on(scalars[0], got["own_pair"][h], got["first"][h]))
    got["second"] = send(passed, second_source)
    got["first_pair"] = send(got["first"], pair_source)
    got["second_pair"] = send(got["second"], pair_source)
    for h in heads:
        here = slice(2 * h, 2 * h + 2)
        flat[here] = step((h,), PIECES[:1], (), False, 0, *flat[here])
    out = ()
    for h in heads:
        state, pieces = flat[2 * h : 2 * h + 2], PIECES[1:]
        if h < heads[-1]:
            state, pieces = step((h,), pieces[:1], sink_args, False, 0, *state), pieces[1:]
        late = () if h < heads[-1] else sink_args
        out = (step((h,), pieces, late, False, 2 if h else 1, *state, *out),)
    return out[0][None]


def solution(mesh):
    placed = (P("ctx", None, "kvh", None), P("kvh", "ctx", None), P("kvh", "ctx", None), P())
    return jax.shard_map(body, mesh=mesh, in_specs=placed, out_specs=P("ctx", None, "kvh", None), check_vma=False)
```
